32 devices in a mesh: groups: 2 (over y), blk: 4 (over z), comp: 2 (over x), lat: 2 (over core).
Axes of the slice: x: 2, y: 2, z: 4, core: 2. Of those that a mesh axis runs over, the one named last changes fastest.
Arguments:
- rhs: float32 [96, 2, 4, 2048], P(('groups', 'comp'), None, 'blk'), parts along dimension 0, may hold values from -6 to 6
- legendre: bfloat16 [4, 2048, 32], P('blk', None, 'lat'), may hold values from -0.03125 to 0.03125
- beam: float32 [24, 2048], replicated, may hold values from 0.3 to 1
- mixing: float32 [24, 48], P(None, 'comp'), may hold values from -0.875 to 0.875
- prior: float32 [48, 2048], P('comp'), may hold values from 0.5 to 4
- inv_noise: float32 [24, 32, 4096], P('comp', ('blk', 'lat')), may hold values from 0.25 to 4
- mask_flags: int32 [24, 32], P('comp', ('blk', 'lat')), may hold values 0 or 1
- cycle_len: int32 [32], P('lat'), may hold values from 16 to 4096, as said below
- cycle_slot: int32 [32], P('lat'), may hold values from 0 to 15, as said below
- m_values: int32 [4], replicated, may hold values from 0 to 2047, as said below
Outputs:
- solution: float32 [96, 2, 4, 2048], P(('groups', 'comp'), None, 'blk'), parts along dimension 0
- residual: float32 [96, 2, 4, 2048], P(('groups', 'comp'), None, 'blk'), parts along dimension 0
The draws below stay inside these ranges and needn't reach their ends.
There are 2 independent parts, one for each index of `groups`. The reference program is written for one: setup_inputs(seed, part) draws one part's arguments, and reference() takes and returns one part's arrays. A program takes and returns all parts, laid end to end along the dimension named above; an argument that names none is the same for every part. Nothing has to cross between parts.
Inputs may be any that keep to these rules, and one draw needn't show every extreme that they name: `cycle_len`: lengths are multiples of 4; each band (aligned block of 16 entries) holds a cycle of exactly 4096 pixels. `cycle_slot`: each aligned block of 16 entries is a permutation of 0 to 15. `m_values`: the m values are distinct, and both 0 and 2047 occur.
All inputs are finite; a program needn't handle non-finite values. No bound on the sum of `mask_flags` on one device may be relied on, other than what follows from the above.
Results may differ from the reference program's by a relative error of at most 0.023.
Values may be sent and summed in bfloat16 or wider, within the bound.
A program may use at most 64 MiB of HBM per device.

```python
import math
import jax
import jax.numpy as jnp
from jax import lax

L = 2048
C = 48
F = 24
PMAX = 4096
R_DEV = 4
ITERS = 3
RB = 16
CYCLES = 32
M_TOT = 4
N_LAT = 2


def draw_cycle_len(key, part):
    quarter = PMAX // 4
    draw_one = jax.random.randint(jax.random.fold_in(key, 11), (CYCLES,), 1, quarter + 1)
    draw_two = jax.random.randint(jax.random.fold_in(key, 12), (CYCLES,), 1, quarter + 1)
    lengths = 4 * jnp.maximum(4, jnp.maximum(draw_one, draw_two))
    longest = jax.random.randint(jax.random.fold_in(key, 13), (CYCLES // RB,), 0, RB)
    positions = jnp.arange(CYCLES, dtype=jnp.int32)
    chosen = positions % RB == jnp.repeat(longest, RB, total_repeat_length=CYCLES)
    return jnp.where(chosen, PMAX, lengths).astype(jnp.int32)


def band_order(band_key):
    return jax.random.permutation(band_key, RB)


def draw_cycle_slot(key, part):
    band_keys = jax.random.split(jax.random.fold_in(key, 21), CYCLES // RB)
    orders = jax.vmap(band_order)(band_keys)
    return orders.reshape(CYCLES).astype(jnp.int32)


def draw_m_values(key, part):
    middle = jax.random.permutation(jax.random.fold_in(key, 31), L - 2)[:M_TOT] + 1
    lowest_at = jax.random.randint(jax.random.fold_in(key, 32), (), 0, M_TOT)
    offset = jax.random.randint(jax.random.fold_in(key, 33), (), 1, M_TOT)
    highest_at = (lowest_at + offset) % M_TOT
    positions = jnp.arange(M_TOT, dtype=jnp.int32)
    values = jnp.where(positions == lowest_at, 0, middle)
    values = jnp.where(positions == highest_at, L - 1, values)
    return values.astype(jnp.int32)


def set_ends(values, stream_key, least, largest):
    spot = [jax.random.randint(jax.random.fold_in(stream_key, axis), (), 0, length) for axis, length in enumerate(values.shape)]
    main_axis = values.shape.index(max(values.shape))
    next_to = spot[:main_axis] + [(spot[main_axis] + 1) % values.shape[main_axis]] + spot[main_axis + 1:]
    return values.at[tuple(spot)].set(least).at[tuple(next_to)].set(largest)


def block_scale(own_key, dims, shards, least, largest):
    level = 1.0
    for dim, parts in shards:
        draws = jax.random.uniform(jax.random.fold_in(jax.random.fold_in(own_key, 6), dim), (parts,), jnp.float32, least / len(shards), largest / len(shards))
        level = level * jnp.repeat(jnp.exp(draws), dims[dim] // parts).reshape((-1,) + (1,) * (len(dims) - 1 - dim))
    return level


def bell_draw(own_key, extent, spread, reach, shards=(), kind=jnp.bfloat16):
    array = spread * jax.random.normal(own_key, extent, jnp.float32)
    if shards:
        array = array * block_scale(own_key, extent, shards, -0.22, 0.18)
    return jnp.clip(array, -reach, reach).astype(kind)


def setup_inputs(seed: int = 0, part: int = 0) -> dict:
    splits = jax.random.split(jax.random.key(seed), 11)
    part_keys = jax.random.split(jax.random.fold_in(splits[10], part), 11)
    rhs = bell_draw(part_keys[0], (C, 2, M_TOT, L), 1.0, 6.0, ((0, 2), (2, 4)), jnp.float32)
    legendre = bell_draw(splits[1], (M_TOT, L, CYCLES), (CYCLES * PMAX // 4) ** -0.5, 0.03125, ((0, 4), (2, 2)))
    beam = jnp.clip(jnp.exp(jax.random.uniform(splits[2], (F, L), jnp.float32, math.log(0.3), math.log(1.0))), 0.3, 1.0)
    mixing = bell_draw(splits[3], (F, C), C ** -0.5, 0.875, ((1, 2),), jnp.float32)
    prior = jnp.clip(jnp.exp(math.log(4.0) - 2.0794415 * jax.random.uniform(splits[4], (C, L), jnp.float32) ** block_scale(splits[4], (C, L), ((0, 2),), -0.2, 0.2)), 0.5, 4.0)
    inv_noise = jnp.clip(jnp.exp(math.log(4.0) - 2.7725887 * jax.random.uniform(splits[5], (F, CYCLES, PMAX), jnp.float32) ** block_scale(splits[5], (F, CYCLES, PMAX), ((0, 2), (1, 8)), -0.2, 0.2)), 0.25, 4.0)
    mask_flags = set_ends((jax.random.randint(splits[6], (F, CYCLES), 0, 8) < 7).astype(jnp.int32), jax.random.fold_in(splits[6], 1), 0, 1)
    cycle_len = draw_cycle_len(jax.random.fold_in(splits[10], 71), part)
    cycle_slot = draw_cycle_slot(jax.random.fold_in(splits[10], 71), part)
    m_values = draw_m_values(jax.random.fold_in(splits[10], 71), part)
    return {"rhs": rhs, "legendre": legendre, "beam": beam, "mixing": mixing, "prior": prior, "inv_noise": inv_noise, "mask_flags": mask_flags, "cycle_len": cycle_len, "cycle_slot": cycle_slot, "m_values": m_values}


HIGHEST_PRECISION = lax.Precision.HIGHEST


def cycle_table(m_values, length):
    pixels = jnp.arange(PMAX, dtype=jnp.int32)
    phase_ids = (m_values[:, None] * (2 * pixels[None, :] + 1)) % (2 * length)
    angles = math.pi * phase_ids.astype(jnp.float32) / length.astype(jnp.float32)
    inside = (pixels < length)[None, :]
    cosine = jnp.where(inside, jnp.cos(angles), jnp.float32(0.0))
    sine_part = jnp.where(inside, -jnp.sin(angles), jnp.float32(0.0))
    return jnp.stack([cosine, sine_part]).astype(jnp.bfloat16)


def slot_columns(cycle_len, cycle_slot):
    slot_ids = jnp.arange(CYCLES, dtype=jnp.int32)
    owners = slot_ids // (N_LAT * R_DEV)
    band_ids = (slot_ids // R_DEV) % N_LAT
    places = slot_ids % R_DEV
    cycle_ids = cycle_slot[band_ids * RB + owners * R_DEV + places]
    columns = (band_ids * RB + cycle_ids).astype(jnp.int32)
    return columns, cycle_len[columns]


def apply_operator(vector, mixing, beam, prior, legendre_slot, inv_noise, mask_flags, lengths, m_values):
    blended = jnp.einsum('fc,ckml->fkml', mixing, vector, precision=HIGHEST_PRECISION)
    blended = (blended * beam[:, None, None, :]).astype(jnp.bfloat16)
    legendre_wide = legendre_slot.astype(jnp.float32)
    coeffs = jnp.einsum('fkml,mlg->fkmg', blended.astype(jnp.float32), legendre_wide,
                        precision=HIGHEST_PRECISION).astype(jnp.bfloat16)

    def one_slot(slot_items):
        coeff_slot, noise_slot, mask_slot, length = slot_items
        trig_table = cycle_table(m_values, length).astype(jnp.float32)
        sky_map = jnp.einsum('fkm,kmp->fp', coeff_slot.astype(jnp.float32), trig_table,
                             precision=HIGHEST_PRECISION)
        weighted = (mask_slot.astype(jnp.float32)[:, None] * noise_slot * sky_map).astype(jnp.bfloat16)
        return jnp.einsum('fp,kmp->fkm', weighted.astype(jnp.float32), trig_table,
                          precision=HIGHEST_PRECISION).astype(jnp.bfloat16)

    projected = lax.map(one_slot, (jnp.moveaxis(coeffs, 3, 0), jnp.moveaxis(inv_noise, 1, 0),
                                   jnp.moveaxis(mask_flags, 1, 0), lengths))
    projected = jnp.moveaxis(projected, 0, 3)
    harmonic = jnp.einsum('fkmg,mlg->fkml', projected.astype(jnp.float32), legendre_wide,
                          precision=HIGHEST_PRECISION)
    backward = jnp.einsum('fc,fkml->ckml', mixing, harmonic * beam[:, None, None, :],
                          precision=HIGHEST_PRECISION)
    return prior[:, None, None, :] * vector + backward


def reference(rhs, legendre, beam, mixing, prior, inv_noise, mask_flags, cycle_len, cycle_slot, m_values):
    columns, lengths = slot_columns(cycle_len, cycle_slot)
    legendre_slot = legendre[:, :, columns]
    solution = jnp.zeros_like(rhs)
    residual = rhs
    direction = rhs
    for iteration in range(ITERS):
        applied = apply_operator(direction, mixing, beam, prior, legendre_slot, inv_noise,
                                 mask_flags, lengths, m_values)
        curvature = jnp.sum(direction * applied)
        cross_term = jnp.sum(residual * applied)
        square = jnp.sum(applied * applied)
        norm_now = jnp.sum(residual * residual)
        step_size = norm_now / curvature
        solution = solution + step_size * direction
        residual = residual - step_size * applied
        norm_next = norm_now - 2.0 * step_size * cross_term + step_size * step_size * square
        direction = residual + (norm_next / norm_now) * direction
    return solution, residual
```

```python
import functools
import math

import jax
import jax.numpy as jnp
from jax import lax
from jax.experimental import pallas as pl
from jax.experimental.pallas import tpu as pltpu
from jax.sharding import PartitionSpec as P

ITERS = 3
F32 = jnp.float32
BF16 = jnp.bfloat16
MESH = pl.DeviceIdType.MESH


def each(count, body):
    if count <= 16:
        for i in range(count):
            body(i)
    else:
        lax.fori_loop(0, count, lambda i, carry: (body(i), carry)[1], 0)


def mm(a, b, ca, cb):
    return lax.dot_general(a, b, (((ca,), (cb,)), ((), ())), preferred_element_type=F32)


def half_turn_trig(turns_num, length, inside):
    j = jnp.floor(2.0 * turns_num / length + 0.5)
    u = (2.0 * turns_num - j * length) / length * (math.pi / 2)
    u2 = u * u
    s = u + u * u2 * (-1.0 / 6 + u2 * (1.0 / 120 + u2 * (-1.0 / 5040 + u2 * (1.0 / 362880))))
    c = 1.0 + u2 * (-0.5 + u2 * (1.0 / 24 + u2 * (-1.0 / 720 + u2 * (1.0 / 40320))))
    odd = (j == 1.0) | (j == 3.0)
    cos_neg = (j == 1.0) | (j == 2.0)
    sin_neg = (j == 2.0) | (j == 3.0)
    cosine = jnp.where(odd, s, c)
    sine = jnp.where(odd, c, s)
    cosine = jnp.where(cos_neg, -cosine, cosine)
    sine = jnp.where(sin_neg, sine, -sine)
    return jnp.where(inside, cosine, 0.0), jnp.where(inside, sine, 0.0)


def kernel(
    dims,
    rhs_ref, leg_ref, beam_ref, mix_ref, mixt_ref, prior_ref, noise_ref, len_ref, slot_ref, m_ref,
    sol_ref, res_ref,
    leg_all, trig, gsend, gbuf, gplane, gt, xsend, xbuf, ssend, sbuf, xd, xr, d_ref, w_ref,
    leg_sems, g_sems, x_sems, s_sems,
):
    nb, nc, nl, fl, fp, qr, rb, mt, lmax, pmax, chunk = dims
    b, c, l = lax.axis_index("blk"), lax.axis_index("comp"), lax.axis_index("lat")
    n_all = nb * nc * nl
    n_x = nb * nc
    me = (b * nc + c) * nl + l
    me_x = b * nc + c
    two_fp = 2 * fp

    def peer_all(k):
        p = lax.rem(me + k, n_all)
        return p // (nc * nl), lax.rem(p // nl, nc), lax.rem(p, nl)

    def peer_x(k):
        p = lax.rem(me_x + k, n_x)
        return p // nc, lax.rem(p, nc)

    barrier = pltpu.get_barrier_semaphore()

    def greet(k):
        pb, pc, pq = peer_all(k + 1)
        pl.semaphore_signal(
            barrier, inc=1, device_id={"blk": pb, "comp": pc, "lat": pq}, device_id_type=MESH
        )

    each(n_all - 1, greet)

    def wait_bytes(ref, sem):
        pltpu.make_async_copy(ref, ref, sem).wait()

    rows = lax.broadcasted_iota(jnp.int32, (rb, rb), 1)
    hot = slot_ref[...] == rows
    own_leg = mm(hot.astype(F32).astype(BF16), leg_ref[...], 1, 1).astype(BF16)
    leg_all[l] = own_leg
    slot_len = jnp.sum(jnp.where(hot, len_ref[...], 0), axis=1, keepdims=True)
    row_ids = lax.broadcasted_iota(jnp.int32, (rb, 1), 0)

    pix = lax.broadcasted_iota(jnp.int32, (mt, pmax), 1)
    whole = m_ref[...] * (2 * pix + 1)
    whole_f = whole.astype(F32)
    for q in range(qr):
        n_i = jnp.sum(jnp.where(row_ids == b * qr + q, slot_len, 0), axis=0, keepdims=True)
        n_f = n_i.astype(F32)
        turns = jnp.floor(whole_f / (2.0 * n_f)).astype(jnp.int32)
        left = whole - turns * (2 * n_i)
        left = jnp.where(left < 0, left + 2 * n_i, left)
        left = jnp.where(left >= 2 * n_i, left - 2 * n_i, left)
        cosine, sine = half_turn_trig(left.astype(F32), n_f, pix < n_i)
        trig[q, 0] = cosine.astype(BF16).astype(F32)
        trig[q, 1] = sine.astype(BF16).astype(F32)

    def gram(m):
        pieces = []
        for q in range(qr):
            co, si = trig[q, 0], trig[q, 1]
            row_c = trig[q, 0, pl.ds(m, 1), :]
            row_s = trig[q, 1, pl.ds(m, 1), :]
            prod = jnp.concatenate([co * row_c, si * row_c, si * row_s, co * row_s], axis=0)
            out = mm(prod.astype(BF16), noise_ref[q], 1, 1)
            pieces += [out[: 2 * mt], out[2 * mt :]]
        width = 2 * qr * fp
        if width < 128:
            pieces.append(jnp.zeros((2 * mt, 128 - width), F32))
        gsend[m] = jnp.concatenate(pieces, axis=1)

    each(mt, gram)

    pl.semaphore_wait(barrier, n_all - 1)

    for k in range(1, nl):
        pltpu.make_async_remote_copy(
            leg_all.at[l], leg_all.at[l], leg_sems.at[0], leg_sems.at[1],
            device_id={"lat": lax.rem(l + k, nl)}, device_id_type=MESH,
        ).start()

    def send_g(k):
        pb, pc, pq = peer_all(k + 1)
        pltpu.make_async_remote_copy(
            gsend.at[pb], gbuf.at[me], g_sems.at[0], g_sems.at[1],
            device_id={"blk": pb, "comp": pc, "lat": pq}, device_id_type=MESH,
        ).start()

    each(n_all - 1, send_g)
    gbuf[me] = gsend[b]

    wait_bytes(leg_all.at[pl.ds(0, nl - 1)], leg_sems.at[1])

    def share_x(r):
        def send(k):
            pb, pc = peer_x(k + 1)
            pltpu.make_async_remote_copy(
                xsend.at[r], xbuf.at[r, me_x], x_sems.at[r, 0], x_sems.at[r, 1],
                device_id={"blk": pb, "comp": pc}, device_id_type=MESH,
            ).start()

        each(n_x - 1, send)
        xbuf[r, me_x] = xsend[r]

    leg_rows = nl * rb
    tile_rows = lax.broadcasted_iota(jnp.int32, (rb, 128), 0)
    tile_lanes = lax.broadcasted_iota(jnp.int32, (rb, 128), 1)
    pad_lane = lax.rem(tile_lanes, fp) >= fl
    first_k = lax.rem(tile_lanes, two_fp) < fp

    def mark(row):
        return (tile_rows == row) & (tile_lanes == fp - 1)

    def forward(values, where, legs, acc):
        bm = beam_ref[:, where]
        parts = [mm(mix_ref[...], v.astype(BF16), 1, 0) * bm for v in values]
        stack = jnp.concatenate(
            [parts[k][i * fp : (i + 1) * fp] for i in range(nc) for k in range(2)], axis=0
        ).astype(BF16)
        return acc + mm(legs, stack, 1, 1)

    def tile_of(acc):
        return jnp.concatenate([acc[i * rb : (i + 1) * rb] for i in range(nl)], axis=1)

    legs_of = lambda where: leg_all[:, :, where].reshape(leg_rows, chunk)

    acc = jnp.zeros((leg_rows, nc * two_fp), F32)
    for ch in range(lmax // chunk):
        where = pl.ds(ch * chunk, chunk)
        values = [rhs_ref[:, pl.ds(k * lmax + ch * chunk, chunk)] for k in range(2)]
        acc = forward(values, where, legs_of(where), acc)
    xsend[0] = tile_of(acc)
    share_x(0)

    wait_bytes(gbuf.at[pl.ds(0, n_all - 1)], g_sems.at[1])

    def place(i):
        for q in range(qr):
            gt[i * qr + q] = jnp.concatenate(
                [
                    gbuf[(i * nc + ic) * nl + il][:, q * two_fp : (q + 1) * two_fp]
                    for il in range(nl)
                    for ic in range(nc)
                ],
                axis=1,
            )

    each(nb, place)
    for p in range(2 * mt):
        gplane[p] = gt[:, p, :]

    def arrive_x(r):
        wait_bytes(xbuf.at[r, pl.ds(0, n_x - 1)], x_sems.at[r, 1])

    def weigh(r, step, ratio):
        def body(m, y):
            x = xbuf[r, m * nc]
            for i in range(1, nc):
                x = x + xbuf[r, m * nc + i]
            x = jnp.where(pad_lane, 0.0, x)
            if r == 0:
                xr[m] = x
                now = x
            else:
                rest = xr[m] - step * x
                now = rest + ratio * xd[m]
                xr[m] = rest
            xd[m] = now
            swapped = jnp.where(
                first_k, pltpu.roll(now, 128 - fp, 1), pltpu.roll(now, fp, 1)
            )
            return y + gplane[m] * now + gplane[mt + m] * swapped

        y = jnp.zeros((rb, 128), F32)
        if mt <= 16:
            for m in range(mt):
                y = body(m, y)
        else:
            y = lax.fori_loop(0, mt, body, y)
        width = nc * two_fp
        return jnp.concatenate(
            [y[:, i * width : (i + 1) * width] for i in range(nl)], axis=0
        ).astype(BF16)

    def total(value):
        return jnp.sum(jnp.sum(value, axis=0, keepdims=True), axis=1, keepdims=True)

    def scalars(tile):
        return [total(jnp.where(mark(i), tile, 0.0)) for i in range(4)]

    def coefficients_of_step(sums):
        curvature, cross, square, norm = sums
        step = norm / curvature
        nxt = norm - 2.0 * step * cross + step * step * square
        return step, nxt / norm

    step = ratio = None
    for it in range(ITERS):
        arrive_x(it)
        if it > 0:
            tile = xbuf[it, 0]
            for i in range(1, n_x):
                tile = tile + xbuf[it, i]
            step, ratio = coefficients_of_step(scalars(tile))
        y = weigh(it, step, ratio)
        last = it == ITERS - 1
        acc = jnp.zeros((leg_rows, nc * two_fp), F32)
        sums = [jnp.zeros((rhs_ref.shape[0], chunk), F32) for _ in range(4)]
        for ch in range(lmax // chunk):
            where = pl.ds(ch * chunk, chunk)
            legs = legs_of(where)
            spread = mm(y, legs, 0, 0)
            bm = beam_ref[:, where]
            values = []
            for k in range(2):
                both = pl.ds(k * lmax + ch * chunk, chunk)
                harm = jnp.concatenate(
                    [spread[i * two_fp + k * fp : i * two_fp + (k + 1) * fp] for i in range(nc)],
                    axis=0,
                )
                back = mm(mixt_ref[...], (harm * bm).astype(BF16), 1, 0)
                if it == 0:
                    d = rhs_ref[:, both]
                    rest = d
                else:
                    old = rhs_ref[:, both] if it == 1 else d_ref[:, both]
                    before = rhs_ref[:, both] if it == 1 else res_ref[:, both]
                    grown = step * old
                    sol_ref[:, both] = grown if it == 1 else sol_ref[:, both] + grown
                    rest = before - step * w_ref[:, both]
                    d = rest + ratio * old
                    res_ref[:, both] = rest
                    d_ref[:, both] = d
                w = prior_ref[:, where] * d + back
                w_ref[:, both] = w
                sums[0] = sums[0] + d * w
                sums[3] = sums[3] + rest * rest
                if not last:
                    sums[1] = sums[1] + rest * w
                    sums[2] = sums[2] + w * w
                values.append(w)
            if not last:
                acc = forward(values, where, legs, acc)
        if not last:
            tile = tile_of(acc)
            for i in range(4):
                tile = jnp.where(mark(i), total(sums[i]), tile)
            xsend[it + 1] = tile
            share_x(it + 1)

    small_rows = lax.broadcasted_iota(jnp.int32, (8, 128), 0)
    ssend[...] = jnp.where(
        small_rows == 0, total(sums[0]), jnp.where(small_rows == 1, total(sums[3]), 0.0)
    )

    def send_s(k):
        pb, pc = peer_x(k + 1)
        pltpu.make_async_remote_copy(
            ssend, sbuf.at[me_x], s_sems.at[0], s_sems.at[1],
            device_id={"blk": pb, "comp": pc}, device_id_type=MESH,
        ).start()

    each(n_x - 1, send_s)
    sbuf[me_x] = ssend[...]
    wait_bytes(sbuf.at[pl.ds(0, n_x - 1)], s_sems.at[1])
    sums = sbuf[0]
    for i in range(1, n_x):
        sums = sums + sbuf[i]
    step = sums[1:2, 0:1] / sums[0:1, 0:1]
    sol_ref[...] = sol_ref[...] + step * d_ref[...]
    res_ref[...] = res_ref[...] - step * w_ref[...]

    wait_bytes(leg_all.at[pl.ds(0, nl - 1)], leg_sems.at[0])
    wait_bytes(gbuf.at[pl.ds(0, n_all - 1)], g_sems.at[0])
    for r in range(ITERS):
        wait_bytes(xbuf.at[r, pl.ds(0, n_x - 1)], x_sems.at[r, 0])
    wait_bytes(sbuf.at[pl.ds(0, n_x - 1)], s_sems.at[0])


def local(
    rhs, legendre, beam, mixing, prior, inv_noise, mask_flags, cycle_len, cycle_slot, m_values
):
    nb, nc, nl = lax.axis_size("blk"), lax.axis_size("comp"), lax.axis_size("lat")
    fl, qr, pmax = inv_noise.shape
    lmax, rb = legendre.shape[1:]
    mt = m_values.shape[0]
    comps = rhs.shape[0]
    fp = 8 * (fl // 8 + 1)
    chunk = min(512, lmax)
    dims = (nb, nc, nl, fl, fp, qr, rb, mt, lmax, pmax, chunk)
    spare = ((0, 0), (0, fp - fl), (0, 0))
    beam_p = jnp.pad(beam.reshape(nc, fl, lmax), spare).reshape(nc * fp, lmax)
    mix_p = jnp.pad(mixing.reshape(nc, fl, comps), spare).reshape(nc * fp, comps).astype(BF16)
    noise = mask_flags.astype(F32)[:, :, None] * inv_noise
    noise = jnp.pad(jnp.transpose(noise, (1, 0, 2)), spare).astype(BF16)
    n_all, n_x = nb * nc * nl, nb * nc
    vm = pl.BlockSpec(memory_space=pltpu.VMEM)
    flat = jax.ShapeDtypeStruct((comps, 2 * lmax), F32)
    sol, res = pl.pallas_call(
        functools.partial(kernel, dims),
        out_shape=(flat, flat),
        in_specs=[vm] * 10,
        out_specs=(vm, vm),
        scratch_shapes=[
            pltpu.VMEM((nl, rb, lmax), BF16),
            pltpu.VMEM((qr, 2, mt, pmax), F32),
            pltpu.VMEM((mt, 2 * mt, 128), F32),
            pltpu.VMEM((n_all, 2 * mt, 128), F32),
            pltpu.VMEM((2 * mt, rb, 128), F32),
            pltpu.VMEM((rb, 2 * mt, 128), F32),
            pltpu.VMEM((ITERS, rb, 128), F32),
            pltpu.VMEM((ITERS, n_x, rb, 128), F32),
            pltpu.VMEM((8, 128), F32),
            pltpu.VMEM((n_x, 8, 128), F32),
            pltpu.VMEM((mt, rb, 128), F32),
            pltpu.VMEM((mt, rb, 128), F32),
            pltpu.VMEM((comps, 2 * lmax), F32),
            pltpu.VMEM((comps, 2 * lmax), F32),
            pltpu.SemaphoreType.DMA((2,)),
            pltpu.SemaphoreType.DMA((2,)),
            pltpu.SemaphoreType.DMA((ITERS, 2)),
            pltpu.SemaphoreType.DMA((2,)),
        ],
        compiler_params=pltpu.CompilerParams(collective_id=0, has_side_effects=True),
    )(
        rhs.reshape(comps, 2 * lmax),
        legendre[0],
        beam_p,
        mix_p,
        mix_p.T,
        prior,
        noise,
        cycle_len[None, :],
        cycle_slot[:, None],
        m_values[:, None],
    )
    return sol.reshape(rhs.shape), res.reshape(rhs.shape)


def solution(mesh):
    in_specs = (
        P(("groups", "comp"), None, "blk", None),
        P("blk", None, "lat"),
        P(),
        P(None, "comp"),
        P("comp", None),
        P("comp", ("blk", "lat"), None),
        P("comp", ("blk", "lat")),
        P("lat"),
        P("lat"),
        P(),
    )
    out_specs = (P(("groups", "comp"), None, "blk", None), P(("groups", "comp"), None, "blk", None))
    return jax.shard_map(local, mesh=mesh, in_specs=in_specs, out_specs=out_specs, check_vma=False)
```

```python
import functools
import math

import jax
import jax.numpy as jnp
from jax import lax
from jax.experimental import pallas as pl
from jax.experimental.pallas import tpu as pltpu
from jax.sharding import PartitionSpec as P

ITERS = 3
F32 = jnp.float32
BF16 = jnp.bfloat16
MESH = pl.DeviceIdType.MESH


def each(count, body):
    if count <= 16:
        for i in range(count):
            body(i)
    else:
        lax.fori_loop(0, count, lambda i, carry: (body(i), carry)[1], 0)


def mm(a, b, ca, cb):
    return lax.dot_general(a, b, (((ca,), (cb,)), ((), ())), preferred_element_type=F32)


def half_turn_trig(turns_num, length, inside):
    j = jnp.floor(2.0 * turns_num / length + 0.5)
    u = (2.0 * turns_num - j * length) / length * (math.pi / 2)
    u2 = u * u
    s = u + u * u2 * (-1.0 / 6 + u2 * (1.0 / 120 + u2 * (-1.0 / 5040 + u2 * (1.0 / 362880))))
    c = 1.0 + u2 * (-0.5 + u2 * (1.0 / 24 + u2 * (-1.0 / 720 + u2 * (1.0 / 40320))))
    odd = (j == 1.0) | (j == 3.0)
    cos_neg = (j == 1.0) | (j == 2.0)
    sin_neg = (j == 2.0) | (j == 3.0)
    cosine = jnp.where(odd, s, c)
    sine = jnp.where(odd, c, s)
    cosine = jnp.where(cos_neg, -cosine, cosine)
    sine = jnp.where(sin_neg, sine, -sine)
    return jnp.where(inside, cosine, 0.0), jnp.where(inside, sine, 0.0)


def kernel(
    dims,
    rhs_ref, leg_ref, beam_in, mix_in, prior_ref, noise_ref, mask_ref, len_ref, slot_ref,
    slot_row, m_ref,
    sol_out, res_out,
    beam_ref, mix_pad, rhs_ref2, sol_ref, res_ref, leg_all, trig, noise_pad, gsend, gbuf, gplane, gt, xsend, xbuf, ssend, sbuf, xd, xr, d_ref, w_ref,
    leg_sems, g_sems, x_sems, s_sems,
):
    nb, nc, nl, fl, fp, qr, rb, mt, lmax, pmax, chunk = dims
    b, c, l = lax.axis_index("blk"), lax.axis_index("comp"), lax.axis_index("lat")
    n_all = nb * nc * nl
    n_x = nb * nc
    me = (b * nc + c) * nl + l
    me_x = b * nc + c
    two_fp = 2 * fp

    def peer_all(k):
        p = lax.rem(me + k, n_all)
        return p // (nc * nl), lax.rem(p // nl, nc), lax.rem(p, nl)

    def peer_x(k):
        p = lax.rem(me_x + k, n_x)
        return p // nc, lax.rem(p, nc)

    barrier = pltpu.get_barrier_semaphore()

    def greet(k):
        pb, pc, pq = peer_all(k + 1)
        pl.semaphore_signal(
            barrier, inc=1, device_id={"blk": pb, "comp": pc, "lat": pq}, device_id_type=MESH
        )

    each(n_all - 1, greet)

    def wait_bytes(ref, sem):
        pltpu.make_async_copy(ref, ref, sem).wait()

    hot = slot_row[...] == lax.broadcasted_iota(jnp.int32, (rb, rb), 0)
    leg_all[l] = mm(hot.astype(F32).astype(BF16), leg_ref[...], 0, 0).astype(BF16)

    beam_ref[...] = jnp.zeros_like(beam_ref)
    mix_pad[...] = jnp.zeros_like(mix_pad)
    for i in range(nc):
        beam_ref[i * fp : i * fp + fl] = beam_in[i * fl : (i + 1) * fl]
        mix_pad[i * fp : i * fp + fl] = mix_in[i * fl : (i + 1) * fl]
    mix = mix_pad[...].astype(BF16)
    rows_p = nc * fp
    eye = lax.broadcasted_iota(jnp.int32, (rows_p, rows_p), 0) == lax.broadcasted_iota(
        jnp.int32, (rows_p, rows_p), 1
    )
    mixt = mm(mix, eye.astype(F32).astype(BF16), 0, 0).astype(BF16)

    def lane_block(k, at):
        return (k * lmax + at) // 128

    pix = lax.broadcasted_iota(jnp.int32, (mt, pmax), 1)
    m_rows = lax.broadcasted_iota(jnp.int32, (mt, 1), 0)
    m_col = jnp.zeros((mt, 1), jnp.int32)
    for m in range(mt):
        m_col = jnp.where(m_rows == m, m_ref[m], m_col)
    whole = m_col * (2 * pix + 1)
    whole_f = whole.astype(F32)
    for q in range(qr):
        n_i = jnp.full((1, 1), len_ref[slot_ref[b * qr + q]], jnp.int32)
        n_f = n_i.astype(F32)
        noise_q = jnp.concatenate(
            [noise_ref[:, q, :], jnp.zeros((fp - fl, pmax), F32)], axis=0
        )
        noise_pad[q] = noise_q.astype(BF16)
        turns = jnp.floor(whole_f / (2.0 * n_f)).astype(jnp.int32)
        left = whole - turns * (2 * n_i)
        left = jnp.where(left < 0, left + 2 * n_i, left)
        left = jnp.where(left >= 2 * n_i, left - 2 * n_i, left)
        cosine, sine = half_turn_trig(left.astype(F32), n_f, pix < n_i)
        trig[q, 0] = cosine.astype(BF16).astype(F32)
        trig[q, 1] = sine.astype(BF16).astype(F32)

    masks = [
        jnp.concatenate(
            [mask_ref[q : q + 1, :].astype(F32), jnp.zeros((1, fp - fl), F32)], axis=1
        )
        for q in range(qr)
    ]

    def gram(m):
        pieces = []
        for q in range(qr):
            co, si = trig[q, 0], trig[q, 1]
            row_c = trig[q, 0, pl.ds(m, 1), :]
            row_s = trig[q, 1, pl.ds(m, 1), :]
            prod = jnp.concatenate([co * row_c, si * row_c, si * row_s, co * row_s], axis=0)
            out = mm(prod.astype(BF16), noise_pad[q], 1, 1) * masks[q]
            pieces += [out[: 2 * mt], out[2 * mt :]]
        width = 2 * qr * fp
        if width < 128:
            pieces.append(jnp.zeros((2 * mt, 128 - width), F32))
        gsend[m] = jnp.concatenate(pieces, axis=1)

    each(mt, gram)

    pl.semaphore_wait(barrier, n_all - 1)

    for k in range(1, nl):
        pltpu.make_async_remote_copy(
            leg_all.at[l], leg_all.at[l], leg_sems.at[0], leg_sems.at[1],
            device_id={"lat": lax.rem(l + k, nl)}, device_id_type=MESH,
        ).start()

    def send_g(k):
        pb, pc, pq = peer_all(k + 1)
        pltpu.make_async_remote_copy(
            gsend.at[pb], gbuf.at[me], g_sems.at[0], g_sems.at[1],
            device_id={"blk": pb, "comp": pc, "lat": pq}, device_id_type=MESH,
        ).start()

    each(n_all - 1, send_g)
    gbuf[me] = gsend[b]

    wait_bytes(leg_all.at[pl.ds(0, nl - 1)], leg_sems.at[1])

    def share_x(r):
        def send(k):
            pb, pc = peer_x(k + 1)
            pltpu.make_async_remote_copy(
                xsend.at[r], xbuf.at[r, me_x], x_sems.at[r, 0], x_sems.at[r, 1],
                device_id={"blk": pb, "comp": pc}, device_id_type=MESH,
            ).start()

        each(n_x - 1, send)
        xbuf[r, me_x] = xsend[r]

    leg_rows = nl * rb
    tile_rows = lax.broadcasted_iota(jnp.int32, (rb, 128), 0)
    tile_lanes = lax.broadcasted_iota(jnp.int32, (rb, 128), 1)
    pad_lane = lax.rem(tile_lanes, fp) >= fl
    first_k = lax.rem(tile_lanes, two_fp) < fp

    def mark(row):
        return (tile_rows == row) & (tile_lanes == fp - 1)

    def forward(values, where, legs, acc):
        bm = beam_ref[:, where]
        parts = [mm(mix, v.astype(BF16), 1, 0) * bm for v in values]
        stack = jnp.concatenate(
            [parts[k][i * fp : (i + 1) * fp] for i in range(nc) for k in range(2)], axis=0
        ).astype(BF16)
        return acc + mm(legs, stack, 1, 1)

    def tile_of(acc):
        return jnp.concatenate([acc[i * rb : (i + 1) * rb] for i in range(nl)], axis=1)

    legs_of = lambda where: leg_all[:, :, where].reshape(leg_rows, chunk)

    acc = jnp.zeros((leg_rows, nc * two_fp), F32)
    for ch in range(lmax // chunk):
        where = pl.ds(ch * chunk, chunk)
        values = []
        for k in range(2):
            at = lane_block(k, ch * chunk)
            v = jnp.concatenate([rhs_ref[:, at + i, :] for i in range(chunk // 128)], axis=1)
            rhs_ref2[:, pl.ds(k * lmax + ch * chunk, chunk)] = v
            values.append(v)
        acc = forward(values, where, legs_of(where), acc)
    xsend[0] = tile_of(acc)
    share_x(0)

    wait_bytes(gbuf.at[pl.ds(0, n_all - 1)], g_sems.at[1])

    def place(i):
        for q in range(qr):
            gt[i * qr + q] = jnp.concatenate(
                [
                    gbuf[(i * nc + ic) * nl + il][:, q * two_fp : (q + 1) * two_fp]
                    for il in range(nl)
                    for ic in range(nc)
                ],
                axis=1,
            )

    each(nb, place)
    for p in range(2 * mt):
        gplane[p] = gt[:, p, :]

    def arrive_x(r):
        wait_bytes(xbuf.at[r, pl.ds(0, n_x - 1)], x_sems.at[r, 1])

    def weigh(r, step, ratio):
        def body(m, y):
            x = xbuf[r, m * nc]
            for i in range(1, nc):
                x = x + xbuf[r, m * nc + i]
            x = jnp.where(pad_lane, 0.0, x)
            if r == 0:
                xr[m] = x
                now = x
            else:
                rest = xr[m] - step * x
                now = rest + ratio * xd[m]
                xr[m] = rest
            xd[m] = now
            swapped = jnp.where(
                first_k, pltpu.roll(now, 128 - fp, 1), pltpu.roll(now, fp, 1)
            )
            return y + gplane[m] * now + gplane[mt + m] * swapped

        y = jnp.zeros((rb, 128), F32)
        if mt <= 16:
            for m in range(mt):
                y = body(m, y)
        else:
            y = lax.fori_loop(0, mt, body, y)
        width = nc * two_fp
        return jnp.concatenate(
            [y[:, i * width : (i + 1) * width] for i in range(nl)], axis=0
        ).astype(BF16)

    def total(value):
        return jnp.sum(jnp.sum(value, axis=0, keepdims=True), axis=1, keepdims=True)

    def scalars(tile):
        return [total(jnp.where(mark(i), tile, 0.0)) for i in range(4)]

    def coefficients_of_step(sums):
        curvature, cross, square, norm = sums
        step = norm / curvature
        nxt = norm - 2.0 * step * cross + step * step * square
        return step, nxt / norm

    step = ratio = None
    for it in range(ITERS):
        arrive_x(it)
        if it > 0:
            tile = xbuf[it, 0]
            for i in range(1, n_x):
                tile = tile + xbuf[it, i]
            step, ratio = coefficients_of_step(scalars(tile))
        y = weigh(it, step, ratio)
        last = it == ITERS - 1
        acc = jnp.zeros((leg_rows, nc * two_fp), F32)
        sums = [jnp.zeros((rhs_ref.shape[0], chunk), F32) for _ in range(4)]
        for ch in range(lmax // chunk):
            where = pl.ds(ch * chunk, chunk)
            legs = legs_of(where)
            spread = mm(y, legs, 0, 0)
            bm = beam_ref[:, where]
            values = []
            for k in range(2):
                both = pl.ds(k * lmax + ch * chunk, chunk)
                harm = jnp.concatenate(
                    [spread[i * two_fp + k * fp : i * two_fp + (k + 1) * fp] for i in range(nc)],
                    axis=0,
                )
                back = mm(mixt, (harm * bm).astype(BF16), 1, 0)
                if it == 0:
                    d = rhs_ref2[:, both]
                    rest = d
                else:
                    old = rhs_ref2[:, both] if it == 1 else d_ref[:, both]
                    before = rhs_ref2[:, both] if it == 1 else res_ref[:, both]
                    grown = step * old
                    sol_ref[:, both] = grown if it == 1 else sol_ref[:, both] + grown
                    rest = before - step * w_ref[:, both]
                    d = rest + ratio * old
                    res_ref[:, both] = rest
                    d_ref[:, both] = d
                w = prior_ref[:, where] * d + back
                w_ref[:, both] = w
                sums[0] = sums[0] + d * w
                sums[3] = sums[3] + rest * rest
                if not last:
                    sums[1] = sums[1] + rest * w
                    sums[2] = sums[2] + w * w
                values.append(w)
            if not last:
                acc = forward(values, where, legs, acc)
        if not last:
            tile = tile_of(acc)
            for i in range(4):
                tile = jnp.where(mark(i), total(sums[i]), tile)
            xsend[it + 1] = tile
            share_x(it + 1)

    small_rows = lax.broadcasted_iota(jnp.int32, (8, 128), 0)
    ssend[...] = jnp.where(
        small_rows == 0, total(sums[0]), jnp.where(small_rows == 1, total(sums[3]), 0.0)
    )

    def send_s(k):
        pb, pc = peer_x(k + 1)
        pltpu.make_async_remote_copy(
            ssend, sbuf.at[me_x], s_sems.at[0], s_sems.at[1],
            device_id={"blk": pb, "comp": pc}, device_id_type=MESH,
        ).start()

    each(n_x - 1, send_s)
    sbuf[me_x] = ssend[...]
    wait_bytes(sbuf.at[pl.ds(0, n_x - 1)], s_sems.at[1])
    sums = sbuf[0]
    for i in range(1, n_x):
        sums = sums + sbuf[i]
    step = sums[1:2, 0:1] / sums[0:1, 0:1]
    for at in range(2 * lmax // 128):
        lanes = pl.ds(at * 128, 128)
        sol_out[:, at, :] = sol_ref[:, lanes] + step * d_ref[:, lanes]
        res_out[:, at, :] = res_ref[:, lanes] - step * w_ref[:, lanes]

    wait_bytes(leg_all.at[pl.ds(0, nl - 1)], leg_sems.at[0])
    wait_bytes(gbuf.at[pl.ds(0, n_all - 1)], g_sems.at[0])
    for r in range(ITERS):
        wait_bytes(xbuf.at[r, pl.ds(0, n_x - 1)], x_sems.at[r, 0])
    wait_bytes(sbuf.at[pl.ds(0, n_x - 1)], s_sems.at[0])


def local(
    rhs, legendre, beam, mixing, prior, inv_noise, mask_flags, cycle_len, cycle_slot, m_values
):
    nb, nc, nl = lax.axis_size("blk"), lax.axis_size("comp"), lax.axis_size("lat")
    fl, qr, pmax = inv_noise.shape
    lmax, rb = legendre.shape[1:]
    mt = m_values.shape[0]
    comps = rhs.shape[0]
    fp = 8 * (fl // 8 + 1)
    chunk = min(512, lmax)
    dims = (nb, nc, nl, fl, fp, qr, rb, mt, lmax, pmax, chunk)
    n_all, n_x = nb * nc * nl, nb * nc
    vm = pl.BlockSpec(memory_space=pltpu.VMEM)
    sm = pl.BlockSpec(memory_space=pltpu.SMEM)
    flat = jax.ShapeDtypeStruct((comps, 2 * lmax // 128, 128), F32)
    sol, res = pl.pallas_call(
        functools.partial(kernel, dims),
        out_shape=(flat, flat),
        in_specs=[vm] * 7 + [sm, sm, vm, sm],
        out_specs=(vm, vm),
        scratch_shapes=[
            pltpu.VMEM((nc * fp, lmax), F32),
            pltpu.VMEM((nc * fp, comps), F32),
            pltpu.VMEM((comps, 2 * lmax), F32),
            pltpu.VMEM((comps, 2 * lmax), F32),
            pltpu.VMEM((comps, 2 * lmax), F32),
            pltpu.VMEM((nl, rb, lmax), BF16),
            pltpu.VMEM((qr, 2, mt, pmax), F32),
            pltpu.VMEM((qr, fp, pmax), BF16),
            pltpu.VMEM((mt, 2 * mt, 128), F32),
            pltpu.VMEM((n_all, 2 * mt, 128), F32),
            pltpu.VMEM((2 * mt, rb, 128), F32),
            pltpu.VMEM((rb, 2 * mt, 128), F32),
            pltpu.VMEM((ITERS, rb, 128), F32),
            pltpu.VMEM((ITERS, n_x, rb, 128), F32),
            pltpu.VMEM((8, 128), F32),
            pltpu.VMEM((n_x, 8, 128), F32),
            pltpu.VMEM((mt, rb, 128), F32),
            pltpu.VMEM((mt, rb, 128), F32),
            pltpu.VMEM((comps, 2 * lmax), F32),
            pltpu.VMEM((comps, 2 * lmax), F32),
            pltpu.SemaphoreType.DMA((2,)),
            pltpu.SemaphoreType.DMA((2,)),
            pltpu.SemaphoreType.DMA((ITERS, 2)),
            pltpu.SemaphoreType.DMA((2,)),
        ],
        compiler_params=pltpu.CompilerParams(collective_id=0, has_side_effects=True),
    )(
        rhs.reshape(comps, 2 * lmax // 128, 128),
        legendre[0].T,
        beam,
        mixing,
        prior,
        inv_noise,
        mask_flags.T,
        cycle_len,
        cycle_slot,
        cycle_slot[None, :],
        m_values,
    )
    return sol.reshape(rhs.shape), res.reshape(rhs.shape)


def solution(mesh):
    in_specs = (
        P(("groups", "comp"), None, "blk", None),
        P("blk", None, "lat"),
        P(),
        P(None, "comp"),
        P("comp", None),
        P("comp", ("blk", "lat"), None),
        P("comp", ("blk", "lat")),
        P("lat"),
        P("lat"),
        P(),
    )
    out_specs = (P(("groups", "comp"), None, "blk", None), P(("groups", "comp"), None, "blk", None))
    return jax.shard_map(local, mesh=mesh, in_specs=in_specs, out_specs=out_specs, check_vma=False)
```

```python
import functools
import math

import jax
import jax.numpy as jnp
from jax import lax
from jax.experimental import pallas as pl
from jax.experimental.pallas import tpu as pltpu
from jax.sharding import PartitionSpec as P

ITERS = 3
F32 = jnp.float32
BF16 = jnp.bfloat16
MESH = pl.DeviceIdType.MESH


def each(count, body):
    if count <= 16:
        for i in range(count):
            body(i)
    else:
        lax.fori_loop(0, count, lambda i, carry: (body(i), carry)[1], 0)


def mm(a, b, ca, cb):
    return lax.dot_general(a, b, (((ca,), (cb,)), ((), ())), preferred_element_type=F32)


def half_turn_trig(turns_num, length, inside):
    j = jnp.floor(2.0 * turns_num / length + 0.5)
    u = (2.0 * turns_num - j * length) / length * (math.pi / 2)
    u2 = u * u
    s = u + u * u2 * (-1.0 / 6 + u2 * (1.0 / 120 + u2 * (-1.0 / 5040 + u2 * (1.0 / 362880))))
    c = 1.0 + u2 * (-0.5 + u2 * (1.0 / 24 + u2 * (-1.0 / 720 + u2 * (1.0 / 40320))))
    odd = (j == 1.0) | (j == 3.0)
    cos_neg = (j == 1.0) | (j == 2.0)
    sin_neg = (j == 2.0) | (j == 3.0)
    cosine = jnp.where(odd, s, c)
    sine = jnp.where(odd, c, s)
    cosine = jnp.where(cos_neg, -cosine, cosine)
    sine = jnp.where(sin_neg, sine, -sine)
    return jnp.where(inside, cosine, 0.0), jnp.where(inside, sine, 0.0)


def kernel(
    dims,
    rhs_ref, leg_ref, beam_in, mix_in, prior_ref, noise_ref, mask_ref, len_ref, slot_ref,
    slot_row, m_ref,
    sol_out, res_out,
    beam_ref, mix_pad, rhs_ref2, sol_ref, res_ref, leg_all, trig, noise_pad, gsend, gbuf, gplane, gt, gall, gfull, gtf, gpf, hsend, hbuf, xsend, xbuf, ssend, sbuf, xd, xr, d_ref, w_ref,
    leg_sems, g_sems, h_sems, f_sems, x_sems, s_sems,
):
    nb, nc, nl, fl, fp, qr, rb, mt, lmax, pmax, chunk, lean = dims
    b, c, l = lax.axis_index("blk"), lax.axis_index("comp"), lax.axis_index("lat")
    n_all = nb * nc * nl
    n_x = nb * nc
    me = (b * nc + c) * nl + l
    me_x = b * nc + c
    two_fp = 2 * fp

    def peer_all(k):
        p = lax.rem(me + k, n_all)
        return p // (nc * nl), lax.rem(p // nl, nc), lax.rem(p, nl)

    def peer_x(k):
        p = lax.rem(me_x + k, n_x)
        return p // nc, lax.rem(p, nc)

    barrier = pltpu.get_barrier_semaphore()

    def greet(k):
        pb, pc, pq = peer_all(k + 1)
        pl.semaphore_signal(
            barrier, inc=1, device_id={"blk": pb, "comp": pc, "lat": pq}, device_id_type=MESH
        )

    each(n_all - 1, greet)

    def wait_bytes(ref, sem):
        pltpu.make_async_copy(ref, ref, sem).wait()

    hot = slot_row[...] == lax.broadcasted_iota(jnp.int32, (rb, rb), 0)
    leg_all[l] = mm(hot.astype(F32).astype(BF16), leg_ref[...], 0, 0).astype(BF16)

    beam_ref[...] = jnp.zeros_like(beam_ref)
    mix_pad[...] = jnp.zeros_like(mix_pad)
    for i in range(nc):
        beam_ref[i * fp : i * fp + fl] = beam_in[i * fl : (i + 1) * fl]
        mix_pad[i * fp : i * fp + fl] = mix_in[i * fl : (i + 1) * fl]
    mix = mix_pad[...].astype(BF16)
    rows_p = nc * fp
    eye = lax.broadcasted_iota(jnp.int32, (rows_p, rows_p), 0) == lax.broadcasted_iota(
        jnp.int32, (rows_p, rows_p), 1
    )
    mixt = mm(mix, eye.astype(F32).astype(BF16), 0, 0).astype(BF16)

    def lane_block(k, at):
        return (k * lmax + at) // 128

    pix = lax.broadcasted_iota(jnp.int32, (mt, pmax), 1)
    m_rows = lax.broadcasted_iota(jnp.int32, (mt, 1), 0)
    m_col = jnp.zeros((mt, 1), jnp.int32)
    for m in range(mt):
        m_col = jnp.where(m_rows == m, m_ref[m], m_col)
    whole = m_col * (2 * pix + 1)
    whole_f = whole.astype(F32)
    for q in range(qr):
        n_i = jnp.full((1, 1), len_ref[slot_ref[b * qr + q]], jnp.int32)
        n_f = n_i.astype(F32)
        noise_q = jnp.concatenate(
            [noise_ref[:, q, :], jnp.zeros((fp - fl, pmax), F32)], axis=0
        )
        noise_pad[q] = noise_q.astype(BF16)
        turns = jnp.floor(whole_f / (2.0 * n_f)).astype(jnp.int32)
        left = whole - turns * (2 * n_i)
        left = jnp.where(left < 0, left + 2 * n_i, left)
        left = jnp.where(left >= 2 * n_i, left - 2 * n_i, left)
        cosine, sine = half_turn_trig(left.astype(F32), n_f, pix < n_i)
        trig[q, 0] = cosine.astype(BF16).astype(F32)
        trig[q, 1] = sine.astype(BF16).astype(F32)

    masks = [
        jnp.concatenate(
            [mask_ref[q : q + 1, :].astype(F32), jnp.zeros((1, fp - fl), F32)], axis=1
        )
        for q in range(qr)
    ]

    def gram(m):
        pieces = []
        for q in range(qr):
            co, si = trig[q, 0], trig[q, 1]
            row_c = trig[q, 0, pl.ds(m, 1), :]
            row_s = trig[q, 1, pl.ds(m, 1), :]
            prod = jnp.concatenate([co * row_c, si * row_c, si * row_s, co * row_s], axis=0)
            out = mm(prod.astype(BF16), noise_pad[q], 1, 1) * masks[q]
            pieces += [out[: 2 * mt], out[2 * mt :]]
        width = 2 * qr * fp
        if width < 128:
            pieces.append(jnp.zeros((2 * mt, 128 - width), F32))
        gsend[m] = jnp.concatenate(pieces, axis=1)

    each(mt, gram)

    leg_rows = nl * rb
    tile_rows = lax.broadcasted_iota(jnp.int32, (rb, 128), 0)
    tile_lanes = lax.broadcasted_iota(jnp.int32, (rb, 128), 1)
    pad_lane = lax.rem(tile_lanes, fp) >= fl
    first_k = lax.rem(tile_lanes, two_fp) < fp

    def mark(row):
        return (tile_rows == row) & (tile_lanes == fp - 1)

    def forward(values, where, legs, acc):
        bm = beam_ref[:, where]
        parts = [mm(mix, v.astype(BF16), 1, 0) * bm for v in values]
        stack = jnp.concatenate(
            [parts[k][i * fp : (i + 1) * fp] for i in range(nc) for k in range(2)], axis=0
        ).astype(BF16)
        return acc + mm(legs, stack, 1, 1)

    def tile_of(acc):
        return jnp.concatenate([acc[i * rb : (i + 1) * rb] for i in range(nl)], axis=1)

    legs_of = lambda where: leg_all[:, :, where].reshape(leg_rows, chunk)

    acc = jnp.zeros((rb, nc * two_fp), F32)
    for ch in range(lmax // chunk):
        where = pl.ds(ch * chunk, chunk)
        values = []
        for k in range(2):
            at = lane_block(k, ch * chunk)
            v = jnp.concatenate([rhs_ref[:, at + i, :] for i in range(chunk // 128)], axis=1)
            rhs_ref2[:, pl.ds(k * lmax + ch * chunk, chunk)] = v
            values.append(v)
        acc = forward(values, where, leg_all[l, :, where], acc)
    part = rb // nl
    hsend[...] = jnp.concatenate([acc[i * part : (i + 1) * part] for i in range(nl)], axis=1)

    pl.semaphore_wait(barrier, n_all - 1)

    for k in range(1, nl):
        pltpu.make_async_remote_copy(
            leg_all.at[l], leg_all.at[l], leg_sems.at[0], leg_sems.at[1],
            device_id={"lat": lax.rem(l + k, nl)}, device_id_type=MESH,
        ).start()

    def send_g(k):
        pb, pc, pq = peer_all(k + 1)
        pltpu.make_async_remote_copy(
            gsend.at[pb], gbuf.at[me], g_sems.at[0], g_sems.at[1],
            device_id={"blk": pb, "comp": pc, "lat": pq}, device_id_type=MESH,
        ).start()
        pltpu.make_async_remote_copy(
            hsend, hbuf.at[me], h_sems.at[0], h_sems.at[1],
            device_id={"blk": pb, "comp": pc, "lat": pq}, device_id_type=MESH,
        ).start()

    each(n_all - 1, send_g)
    gbuf[me] = gsend[b]
    hbuf[me] = hsend[...]

    if lean:
        for m in range(mt):
            gall[m * 2 * mt : (m + 1) * 2 * mt] = gsend[m]
        gfull[me_x] = gall[...].astype(BF16)

    def share_x(r):
        def send(k):
            pb, pc = peer_x(k + 1)
            pltpu.make_async_remote_copy(
                xsend.at[r - 1], xbuf.at[r - 1, me_x], x_sems.at[r - 1, 0], x_sems.at[r - 1, 1],
                device_id={"blk": pb, "comp": pc}, device_id_type=MESH,
            ).start()

        each(n_x - 1, send)
        xbuf[r - 1, me_x] = xsend[r - 1]

    wait_bytes(gbuf.at[pl.ds(0, n_all - 1)], g_sems.at[1])

    def place(i):
        for q in range(qr):
            gt[i * qr + q] = jnp.concatenate(
                [
                    gbuf[(i * nc + ic) * nl + il][:, q * two_fp : (q + 1) * two_fp]
                    for il in range(nl)
                    for ic in range(nc)
                ],
                axis=1,
            )

    each(nb, place)
    for p in range(2 * mt):
        gplane[p] = gt[:, p, :]

    def send_full():
        def send(k):
            pb, pc = peer_x(k + 1)
            pltpu.make_async_remote_copy(
                gfull.at[me_x], gfull.at[me_x], f_sems.at[0], f_sems.at[1],
                device_id={"blk": pb, "comp": pc}, device_id_type=MESH,
            ).start()

        each(n_x - 1, send)

    def place_full():
        wait_bytes(gfull.at[pl.ds(0, n_x - 1)], f_sems.at[1])
        for i in range(nb):
            tiles = [gfull[i * nc + ic].astype(F32) for ic in range(nc)]
            for q in range(qr):
                pieces = [t[:, q * two_fp : (q + 1) * two_fp] for t in tiles]
                pieces.append(jnp.zeros((2 * mt * mt, 128 - nc * two_fp), F32))
                gtf[i * qr + q] = jnp.concatenate(pieces, axis=1)
        for p in range(2 * mt * mt):
            gpf[p] = gtf[:, p, :]

    def own_band_form():
        width = nc * two_fp
        own = []
        for m in range(mt):
            x = xd[m]
            for i in range(1, nl):
                x = jnp.where(l == i, pltpu.roll(xd[m], 128 - i * width, 1), x)
            own.append(x)
        swapped = [
            jnp.where(first_k, pltpu.roll(x, 128 - fp, 1), pltpu.roll(x, fp, 1)) for x in own
        ]
        form = jnp.zeros((rb, 128), F32)
        for m in range(mt):
            y = jnp.zeros((rb, 128), F32)
            for o in range(mt):
                y = y + gpf[m * 2 * mt + o] * own[o] + gpf[m * 2 * mt + mt + o] * swapped[o]
            form = form + y * own[m]
        return total(form)

    def arrive_x(r):
        if r == 0:
            wait_bytes(hbuf.at[pl.ds(0, n_all - 1)], h_sems.at[1])
        else:
            wait_bytes(xbuf.at[r - 1, pl.ds(0, n_x - 1)], x_sems.at[r - 1, 1])

    def first_tile(m):
        bands = []
        for il in range(nl):
            t = hbuf[(m * nc) * nl + il]
            for ic in range(1, nc):
                t = t + hbuf[(m * nc + ic) * nl + il]
            width = nc * two_fp
            bands.append(
                jnp.concatenate([t[:, i * width : (i + 1) * width] for i in range(nl)], axis=0)
            )
        return jnp.concatenate(bands, axis=1)

    def weigh(r, step, ratio):
        def body(m, y):
            if r == 0:
                x = first_tile(m)
            else:
                x = xbuf[r - 1, m * nc]
                for i in range(1, nc):
                    x = x + xbuf[r - 1, m * nc + i]
            x = jnp.where(pad_lane, 0.0, x)
            if r == 0:
                xr[m] = x
                now = x
            else:
                rest = xr[m] - step * x
                now = rest + ratio * xd[m]
                xr[m] = rest
            xd[m] = now
            swapped = jnp.where(
                first_k, pltpu.roll(now, 128 - fp, 1), pltpu.roll(now, fp, 1)
            )
            return y + gplane[m] * now + gplane[mt + m] * swapped

        y = jnp.zeros((rb, 128), F32)
        if mt <= 16:
            for m in range(mt):
                y = body(m, y)
        else:
            y = lax.fori_loop(0, mt, body, y)
        width = nc * two_fp
        return jnp.concatenate(
            [y[:, i * width : (i + 1) * width] for i in range(nl)], axis=0
        ).astype(BF16)

    def fold(value):
        out = value[:, :128]
        for i in range(1, value.shape[1] // 128):
            out = out + value[:, i * 128 : (i + 1) * 128]
        return out

    def total(value):
        return jnp.sum(jnp.sum(value, axis=0, keepdims=True), axis=1, keepdims=True)

    def scalars(tile, count):
        return [total(jnp.where(mark(i), tile, 0.0)) for i in range(count)]

    def coefficients_of_step(sums):
        curvature, cross, square, norm = sums[:4]
        step = norm / curvature
        nxt = norm - 2.0 * step * cross + step * step * square
        return step, nxt / norm, nxt

    step = ratio = norm = smooth = None
    for it in range(ITERS):
        arrive_x(it)
        if it > 0:
            tile = xbuf[it - 1, 0]
            for i in range(1, n_x):
                tile = tile + xbuf[it - 1, i]
            sums = scalars(tile, 10 if it == ITERS - 1 and lean else 4)
            step, ratio, norm = coefficients_of_step(sums)
        y = weigh(it, step, ratio)
        last = it == ITERS - 1
        if last and lean:
            rr, ww, dd, rw, rd, wd = sums[4:]
            smooth = (
                rr + step * step * ww + ratio * ratio * dd
                - 2.0 * step * rw + 2.0 * ratio * rd - 2.0 * step * ratio * wd
            )
            form = own_band_form()
            ssend[...] = jnp.broadcast_to(form, (8, 128))
            for k in range(1, nl):
                pltpu.make_async_remote_copy(
                    ssend, sbuf.at[l], s_sems.at[0], s_sems.at[1],
                    device_id={"lat": lax.rem(l + k, nl)}, device_id_type=MESH,
                ).start()
            sbuf[l] = ssend[...]
        acc = jnp.zeros((leg_rows, nc * two_fp), F32)
        weighted = lean and it == ITERS - 2
        sums = [jnp.zeros((rhs_ref.shape[0], 128), F32) for _ in range(10 if weighted else 4)]
        if it == 0:
            wait_bytes(leg_all.at[pl.ds(0, nl - 1)], leg_sems.at[1])
        for ch in range(lmax // chunk):
            where = pl.ds(ch * chunk, chunk)
            legs = legs_of(where)
            spread = mm(y, legs, 0, 0)
            bm = beam_ref[:, where]
            values = []
            for k in range(2):
                both = pl.ds(k * lmax + ch * chunk, chunk)
                harm = jnp.concatenate(
                    [spread[i * two_fp + k * fp : i * two_fp + (k + 1) * fp] for i in range(nc)],
                    axis=0,
                )
                back = mm(mixt, (harm * bm).astype(BF16), 1, 0)
                if it == 0:
                    d = rhs_ref2[:, both]
                    rest = d
                else:
                    old = rhs_ref2[:, both] if it == 1 else d_ref[:, both]
                    before = rhs_ref2[:, both] if it == 1 else res_ref[:, both]
                    grown = step * old
                    sol_ref[:, both] = grown if it == 1 else sol_ref[:, both] + grown
                    rest = before - step * w_ref[:, both]
                    d = rest + ratio * old
                    res_ref[:, both] = rest
                    d_ref[:, both] = d
                w = prior_ref[:, where] * d + back
                w_ref[:, both] = w
                if not (last and lean):
                    sums[0] = sums[0] + fold(d * w)
                    sums[3] = sums[3] + fold(rest * rest)
                if weighted:
                    pr, pw, pd = [prior_ref[:, where] * v for v in (rest, w, d)]
                    for i, v in enumerate(
                        (rest * pr, w * pw, d * pd, rest * pw, rest * pd, w * pd)
                    ):
                        sums[4 + i] = sums[4 + i] + fold(v)
                if not last:
                    sums[1] = sums[1] + fold(rest * w)
                    sums[2] = sums[2] + fold(w * w)
                values.append(w)
            if not last:
                acc = forward(values, where, legs, acc)
        if not last:
            tile = tile_of(acc)
            for i in range(len(sums)):
                tile = jnp.where(mark(i), total(sums[i]), tile)
            xsend[it] = tile
            share_x(it + 1)
            if lean and it == 0:
                send_full()
            if lean and it == ITERS - 2:
                place_full()

    if lean:
        wait_bytes(sbuf.at[pl.ds(0, nl - 1)], s_sems.at[1])
        form = sbuf[0]
        for i in range(1, nl):
            form = form + sbuf[i]
        step = norm / (smooth + form[0:1, 0:1])
    else:
        small_rows = lax.broadcasted_iota(jnp.int32, (8, 128), 0)
        ssend[...] = jnp.where(
            small_rows == 0, total(sums[0]), jnp.where(small_rows == 1, total(sums[3]), 0.0)
        )

        def send_s(k):
            pb, pc = peer_x(k + 1)
            pltpu.make_async_remote_copy(
                ssend, sbuf.at[me_x], s_sems.at[0], s_sems.at[1],
                device_id={"blk": pb, "comp": pc}, device_id_type=MESH,
            ).start()

        each(n_x - 1, send_s)
        sbuf[me_x] = ssend[...]
        wait_bytes(sbuf.at[pl.ds(0, n_x - 1)], s_sems.at[1])
        sums = sbuf[0]
        for i in range(1, n_x):
            sums = sums + sbuf[i]
        step = sums[1:2, 0:1] / sums[0:1, 0:1]
    for at in range(2 * lmax // 128):
        lanes = pl.ds(at * 128, 128)
        sol_out[:, at, :] = sol_ref[:, lanes] + step * d_ref[:, lanes]
        res_out[:, at, :] = res_ref[:, lanes] - step * w_ref[:, lanes]

    wait_bytes(leg_all.at[pl.ds(0, nl - 1)], leg_sems.at[0])
    wait_bytes(gbuf.at[pl.ds(0, n_all - 1)], g_sems.at[0])
    wait_bytes(hbuf.at[pl.ds(0, n_all - 1)], h_sems.at[0])
    for r in range(1, ITERS):
        wait_bytes(xbuf.at[r - 1, pl.ds(0, n_x - 1)], x_sems.at[r - 1, 0])
    if lean:
        wait_bytes(gfull.at[pl.ds(0, n_x - 1)], f_sems.at[0])
        wait_bytes(sbuf.at[pl.ds(0, nl - 1)], s_sems.at[0])
    else:
        wait_bytes(sbuf.at[pl.ds(0, n_x - 1)], s_sems.at[0])


def local(
    rhs, legendre, beam, mixing, prior, inv_noise, mask_flags, cycle_len, cycle_slot, m_values
):
    nb, nc, nl = lax.axis_size("blk"), lax.axis_size("comp"), lax.axis_size("lat")
    fl, qr, pmax = inv_noise.shape
    lmax, rb = legendre.shape[1:]
    mt = m_values.shape[0]
    comps = rhs.shape[0]
    fp = 8 * (fl // 8 + 1)
    chunk = min(512, lmax)
    lean = mt <= 8
    full = 2 * mt * mt if lean else 16
    dims = (nb, nc, nl, fl, fp, qr, rb, mt, lmax, pmax, chunk, lean)
    n_all, n_x = nb * nc * nl, nb * nc
    vm = pl.BlockSpec(memory_space=pltpu.VMEM)
    sm = pl.BlockSpec(memory_space=pltpu.SMEM)
    flat = jax.ShapeDtypeStruct((comps, 2 * lmax // 128, 128), F32)
    sol, res = pl.pallas_call(
        functools.partial(kernel, dims),
        out_shape=(flat, flat),
        in_specs=[vm] * 7 + [sm, sm, vm, sm],
        out_specs=(vm, vm),
        scratch_shapes=[
            pltpu.VMEM((nc * fp, lmax), F32),
            pltpu.VMEM((nc * fp, comps), F32),
            pltpu.VMEM((comps, 2 * lmax), F32),
            pltpu.VMEM((comps, 2 * lmax), F32),
            pltpu.VMEM((comps, 2 * lmax), F32),
            pltpu.VMEM((nl, rb, lmax), BF16),
            pltpu.VMEM((qr, 2, mt, pmax), F32),
            pltpu.VMEM((qr, fp, pmax), BF16),
            pltpu.VMEM((mt, 2 * mt, 128), F32),
            pltpu.VMEM((n_all, 2 * mt, 128), F32),
            pltpu.VMEM((2 * mt, rb, 128), F32),
            pltpu.VMEM((rb, 2 * mt, 128), F32),
            pltpu.VMEM((full, 128), F32),
            pltpu.VMEM((n_x, full, 128), BF16),
            pltpu.VMEM((rb, full, 128), F32),
            pltpu.VMEM((full, rb, 128), F32),
            pltpu.VMEM((rb // nl, 128), F32),
            pltpu.VMEM((n_all, rb // nl, 128), F32),
            pltpu.VMEM((ITERS - 1, rb, 128), F32),
            pltpu.VMEM((ITERS - 1, n_x, rb, 128), F32),
            pltpu.VMEM((8, 128), F32),
            pltpu.VMEM((n_x, 8, 128), F32),
            pltpu.VMEM((mt, rb, 128), F32),
            pltpu.VMEM((mt, rb, 128), F32),
            pltpu.VMEM((comps, 2 * lmax), F32),
            pltpu.VMEM((comps, 2 * lmax), F32),
            pltpu.SemaphoreType.DMA((2,)),
            pltpu.SemaphoreType.DMA((2,)),
            pltpu.SemaphoreType.DMA((2,)),
            pltpu.SemaphoreType.DMA((2,)),
            pltpu.SemaphoreType.DMA((ITERS - 1, 2)),
            pltpu.SemaphoreType.DMA((2,)),
        ],
        compiler_params=pltpu.CompilerParams(collective_id=0, has_side_effects=True),
    )(
        rhs.reshape(comps, 2 * lmax // 128, 128),
        legendre[0].T,
        beam,
        mixing,
        prior,
        inv_noise,
        mask_flags.T,
        cycle_len,
        cycle_slot,
        cycle_slot[None, :],
        m_values,
    )
    return sol.reshape(rhs.shape), res.reshape(rhs.shape)


def solution(mesh):
    in_specs = (
        P(("groups", "comp"), None, "blk", None),
        P("blk", None, "lat"),
        P(),
        P(None, "comp"),
        P("comp", None),
        P("comp", ("blk", "lat"), None),
        P("comp", ("blk", "lat")),
        P("lat"),
        P("lat"),
        P(),
    )
    out_specs = (P(("groups", "comp"), None, "blk", None), P(("groups", "comp"), None, "blk", None))
    return jax.shard_map(local, mesh=mesh, in_specs=in_specs, out_specs=out_specs, check_vma=False)
```

```python
import functools
import math

import jax
import jax.numpy as jnp
from jax import lax
from jax.experimental import pallas as pl
from jax.experimental.pallas import tpu as pltpu
from jax.sharding import PartitionSpec as P

ITERS = 3
F32 = jnp.float32
BF16 = jnp.bfloat16
MESH = pl.DeviceIdType.MESH


def each(count, body):
    if count <= 16:
        for i in range(count):
            body(i)
    else:
        lax.fori_loop(0, count, lambda i, carry: (body(i), carry)[1], 0)


def mm(a, b, ca, cb):
    return lax.dot_general(a, b, (((ca,), (cb,)), ((), ())), preferred_element_type=F32)


def half_turn_trig(turns_num, length, inside):
    j = jnp.floor(2.0 * turns_num / length + 0.5)
    u = (2.0 * turns_num - j * length) / length * (math.pi / 2)
    u2 = u * u
    s = u + u * u2 * (-1.0 / 6 + u2 * (1.0 / 120 + u2 * (-1.0 / 5040 + u2 * (1.0 / 362880))))
    c = 1.0 + u2 * (-0.5 + u2 * (1.0 / 24 + u2 * (-1.0 / 720 + u2 * (1.0 / 40320))))
    odd = (j == 1.0) | (j == 3.0)
    cos_neg = (j == 1.0) | (j == 2.0)
    sin_neg = (j == 2.0) | (j == 3.0)
    cosine = jnp.where(odd, s, c)
    sine = jnp.where(odd, c, s)
    cosine = jnp.where(cos_neg, -cosine, cosine)
    sine = jnp.where(sin_neg, sine, -sine)
    return jnp.where(inside, cosine, 0.0), jnp.where(inside, sine, 0.0)


def kernel(
    dims,
    rhs_ref, leg_ref, beam_in, mix_in, prior_ref, noise_ref, mask_ref, len_ref, slot_ref,
    slot_row, m_ref,
    sol_ref, dir_out, res_ref, w_ref, step_out,
    beam_ref, mix_pad, rhs_ref2, leg_all, trig, noise_pad, gsend, gbuf, gplane, gt, gall, gfull, gtf, gpf, msend, xsend, xbuf, ssend, sbuf, xd, xr, keep,
    leg_sems, g_sems, f_sems, x_sems, s_sems,
):
    nb, nc, nl, fl, fp, qr, rb, mt, lmax, pmax, chunk, lean = dims
    b, c, l = lax.axis_index("blk"), lax.axis_index("comp"), lax.axis_index("lat")
    n_all = nb * nc * nl
    n_x = nb * nc
    me = (b * nc + c) * nl + l
    me_x = b * nc + c
    two_fp = 2 * fp

    def peer_all(k):
        p = lax.rem(me + k, n_all)
        return p // (nc * nl), lax.rem(p // nl, nc), lax.rem(p, nl)

    def peer_x(k):
        p = lax.rem(me_x + k, n_x)
        return p // nc, lax.rem(p, nc)

    barrier = pltpu.get_barrier_semaphore()

    def greet(k):
        pb, pc, pq = peer_all(k + 1)
        pl.semaphore_signal(
            barrier, inc=1, device_id={"blk": pb, "comp": pc, "lat": pq}, device_id_type=MESH
        )

    each(n_all - 1, greet)

    def wait_bytes(ref, sem):
        pltpu.make_async_copy(ref, ref, sem).wait()

    hot = slot_row[...] == lax.broadcasted_iota(jnp.int32, (rb, rb), 0)
    leg_all[l] = mm(hot.astype(F32).astype(BF16), leg_ref[...], 0, 0).astype(BF16)

    beam_ref[...] = jnp.zeros_like(beam_ref)
    mix_pad[...] = jnp.zeros_like(mix_pad)
    for i in range(nc):
        beam_ref[i * fp : i * fp + fl] = beam_in[i * fl : (i + 1) * fl]
        mix_pad[i * fp : i * fp + fl] = mix_in[i * fl : (i + 1) * fl]
    mix = mix_pad[...].astype(BF16)
    rows_p = nc * fp
    eye = lax.broadcasted_iota(jnp.int32, (rows_p, rows_p), 0) == lax.broadcasted_iota(
        jnp.int32, (rows_p, rows_p), 1
    )
    mixt = mm(mix, eye.astype(F32).astype(BF16), 0, 0).astype(BF16)

    def lane_block(k, at):
        return (k * lmax + at) // 128

    pix = lax.broadcasted_iota(jnp.int32, (mt, pmax), 1)
    m_rows = lax.broadcasted_iota(jnp.int32, (mt, 1), 0)
    m_col = jnp.zeros((mt, 1), jnp.int32)
    for m in range(mt):
        m_col = jnp.where(m_rows == m, m_ref[m], m_col)
    whole = m_col * (2 * pix + 1)
    whole_f = whole.astype(F32)
    for q in range(qr):
        n_i = jnp.full((1, 1), len_ref[slot_ref[b * qr + q]], jnp.int32)
        n_f = n_i.astype(F32)
        noise_q = jnp.concatenate(
            [noise_ref[:, q, :], jnp.zeros((fp - fl, pmax), F32)], axis=0
        )
        noise_pad[q] = noise_q.astype(BF16)
        turns = jnp.floor(whole_f / (2.0 * n_f)).astype(jnp.int32)
        left = whole - turns * (2 * n_i)
        left = jnp.where(left < 0, left + 2 * n_i, left)
        left = jnp.where(left >= 2 * n_i, left - 2 * n_i, left)
        cosine, sine = half_turn_trig(left.astype(F32), n_f, pix < n_i)
        trig[q, 0] = cosine.astype(BF16).astype(F32)
        trig[q, 1] = sine.astype(BF16).astype(F32)

    masks = [
        jnp.concatenate(
            [mask_ref[q : q + 1, :].astype(F32), jnp.zeros((1, fp - fl), F32)], axis=1
        )
        for q in range(qr)
    ]

    def gram(m):
        pieces = []
        for q in range(qr):
            co, si = trig[q, 0], trig[q, 1]
            row_c = trig[q, 0, pl.ds(m, 1), :]
            row_s = trig[q, 1, pl.ds(m, 1), :]
            prod = jnp.concatenate([co * row_c, si * row_c, si * row_s, co * row_s], axis=0)
            out = mm(prod.astype(BF16), noise_pad[q], 1, 1) * masks[q]
            pieces += [out[: 2 * mt], out[2 * mt :]]
        width = 2 * qr * fp
        if width < 128:
            pieces.append(jnp.zeros((2 * mt, 128 - width), F32))
        gsend[m] = jnp.concatenate(pieces, axis=1)

    each(mt, gram)

    leg_rows = nl * rb
    tile_rows = lax.broadcasted_iota(jnp.int32, (rb, 128), 0)
    tile_lanes = lax.broadcasted_iota(jnp.int32, (rb, 128), 1)
    pad_lane = lax.rem(tile_lanes, fp) >= fl
    first_k = lax.rem(tile_lanes, two_fp) < fp

    def mark(row):
        return (tile_rows == row) & (tile_lanes == fp - 1)

    def forward(values, where, legs, acc):
        bm = beam_ref[:, where]
        parts = [mm(mix, v.astype(BF16), 1, 0) * bm for v in values]
        stack = jnp.concatenate(
            [parts[k][i * fp : (i + 1) * fp] for i in range(nc) for k in range(2)], axis=0
        ).astype(BF16)
        return acc + mm(legs, stack, 1, 1)

    def tile_of(acc):
        return jnp.concatenate([acc[i * rb : (i + 1) * rb] for i in range(nl)], axis=1)

    legs_of = lambda where: leg_all[:, :, where].reshape(leg_rows, chunk)

    acc = jnp.zeros((rb, nc * two_fp), F32)
    for ch in range(lmax // chunk):
        where = pl.ds(ch * chunk, chunk)
        values = []
        for k in range(2):
            at = lane_block(k, ch * chunk)
            v = jnp.concatenate([rhs_ref[:, at + i, :] for i in range(chunk // 128)], axis=1)
            rhs_ref2[:, pl.ds(k * lmax + ch * chunk, chunk)] = v
            values.append(v)
        acc = forward(values, where, leg_all[l, :, where], acc)
    part = rb // nl
    first = jnp.concatenate([acc[i * part : (i + 1) * part] for i in range(nl)], axis=1)

    def pack(m):
        msend[m] = jnp.concatenate([gsend[m], first], axis=0).astype(BF16)

    each(mt, pack)

    pl.semaphore_wait(barrier, n_all - 1)

    for k in range(1, nl):
        pltpu.make_async_remote_copy(
            leg_all.at[l], leg_all.at[l], leg_sems.at[0], leg_sems.at[1],
            device_id={"lat": lax.rem(l + k, nl)}, device_id_type=MESH,
        ).start()

    def send_g(k):
        pb, pc, pq = peer_all(k + 1)
        pltpu.make_async_remote_copy(
            msend.at[pb], gbuf.at[me], g_sems.at[0], g_sems.at[1],
            device_id={"blk": pb, "comp": pc, "lat": pq}, device_id_type=MESH,
        ).start()

    each(n_all - 1, send_g)
    gbuf[me] = msend[b]

    if lean:
        for m in range(mt):
            gall[m * 2 * mt : (m + 1) * 2 * mt] = gsend[m]
        gfull[me_x] = gall[...].astype(BF16)

    def share_x(r):
        def send(k):
            pb, pc = peer_x(k + 1)
            pltpu.make_async_remote_copy(
                xsend.at[r - 1], xbuf.at[r - 1, me_x], x_sems.at[r - 1, 0], x_sems.at[r - 1, 1],
                device_id={"blk": pb, "comp": pc}, device_id_type=MESH,
            ).start()

        each(n_x - 1, send)
        xbuf[r - 1, me_x] = xsend[r - 1]

    wait_bytes(gbuf.at[pl.ds(0, n_all - 1)], g_sems.at[1])

    def place(i):
        for q in range(qr):
            gt[i * qr + q] = jnp.concatenate(
                [
                    gbuf[(i * nc + ic) * nl + il][: 2 * mt, q * two_fp : (q + 1) * two_fp].astype(F32)
                    for il in range(nl)
                    for ic in range(nc)
                ],
                axis=1,
            )

    each(nb, place)
    for p in range(2 * mt):
        gplane[p] = gt[:, p, :]

    def send_full():
        def send(k):
            pb, pc = peer_x(k + 1)
            pltpu.make_async_remote_copy(
                gfull.at[me_x], gfull.at[me_x], f_sems.at[0], f_sems.at[1],
                device_id={"blk": pb, "comp": pc}, device_id_type=MESH,
            ).start()

        each(n_x - 1, send)

    def place_full():
        wait_bytes(gfull.at[pl.ds(0, n_x - 1)], f_sems.at[1])
        for i in range(nb):
            tiles = [gfull[i * nc + ic].astype(F32) for ic in range(nc)]
            for q in range(qr):
                pieces = [t[:, q * two_fp : (q + 1) * two_fp] for t in tiles]
                pieces.append(jnp.zeros((2 * mt * mt, 128 - nc * two_fp), F32))
                gtf[i * qr + q] = jnp.concatenate(pieces, axis=1)
        for p in range(2 * mt * mt):
            gpf[p] = gtf[:, p, :]

    def own_band_form():
        width = nc * two_fp
        own = []
        for m in range(mt):
            x = xd[m]
            for i in range(1, nl):
                x = jnp.where(l == i, pltpu.roll(xd[m], 128 - i * width, 1), x)
            own.append(x)
        swapped = [
            jnp.where(first_k, pltpu.roll(x, 128 - fp, 1), pltpu.roll(x, fp, 1)) for x in own
        ]
        form = jnp.zeros((rb, 128), F32)
        for m in range(mt):
            y = jnp.zeros((rb, 128), F32)
            for o in range(mt):
                y = y + gpf[m * 2 * mt + o] * own[o] + gpf[m * 2 * mt + mt + o] * swapped[o]
            form = form + y * own[m]
        return total(form)

    def arrive_x(r):
        if r > 0:
            wait_bytes(xbuf.at[r - 1, pl.ds(0, n_x - 1)], x_sems.at[r - 1, 1])

    def first_tile(m):
        bands = []
        for il in range(nl):
            t = gbuf[(m * nc) * nl + il][2 * mt :].astype(F32)
            for ic in range(1, nc):
                t = t + gbuf[(m * nc + ic) * nl + il][2 * mt :].astype(F32)
            width = nc * two_fp
            bands.append(
                jnp.concatenate([t[:, i * width : (i + 1) * width] for i in range(nl)], axis=0)
            )
        return jnp.concatenate(bands, axis=1)

    def weigh(r, step, ratio):
        def body(m, y):
            if r == 0:
                x = first_tile(m)
            else:
                x = xbuf[r - 1, m * nc]
                for i in range(1, nc):
                    x = x + xbuf[r - 1, m * nc + i]
            x = jnp.where(pad_lane, 0.0, x)
            if r == 0:
                xr[m] = x
                now = x
            else:
                rest = xr[m] - step * x
                now = rest + ratio * xd[m]
                xr[m] = rest
            xd[m] = now
            swapped = jnp.where(
                first_k, pltpu.roll(now, 128 - fp, 1), pltpu.roll(now, fp, 1)
            )
            return y + gplane[m] * now + gplane[mt + m] * swapped

        y = jnp.zeros((rb, 128), F32)
        if mt <= 16:
            for m in range(mt):
                y = body(m, y)
        else:
            y = lax.fori_loop(0, mt, body, y)
        width = nc * two_fp
        return jnp.concatenate(
            [y[:, i * width : (i + 1) * width] for i in range(nl)], axis=0
        ).astype(BF16)

    def put(slot, ref, last, both, at, value):
        if not last:
            keep[slot, :, both] = value
            return
        for i in range(chunk // 128):
            ref[:, at + i, :] = value[:, i * 128 : (i + 1) * 128]

    def fold(value):
        out = value[:, :128]
        for i in range(1, value.shape[1] // 128):
            out = out + value[:, i * 128 : (i + 1) * 128]
        return out

    def total(value):
        return jnp.sum(jnp.sum(value, axis=0, keepdims=True), axis=1, keepdims=True)

    def scalars(tile, count):
        return [total(jnp.where(mark(i), tile, 0.0)) for i in range(count)]

    def coefficients_of_step(sums):
        curvature, cross, square, norm = sums[:4]
        step = norm / curvature
        nxt = norm - 2.0 * step * cross + step * step * square
        return step, nxt / norm, nxt

    step = ratio = norm = smooth = None
    for it in range(ITERS):
        arrive_x(it)
        if it > 0:
            tile = xbuf[it - 1, 0]
            for i in range(1, n_x):
                tile = tile + xbuf[it - 1, i]
            sums = scalars(tile, 10 if it == ITERS - 1 and lean else 4)
            step, ratio, norm = coefficients_of_step(sums)
        y = weigh(it, step, ratio)
        last = it == ITERS - 1
        if last and lean:
            rr, ww, dd, rw, rd, wd = sums[4:]
            smooth = (
                rr + step * step * ww + ratio * ratio * dd
                - 2.0 * step * rw + 2.0 * ratio * rd - 2.0 * step * ratio * wd
            )
            form = own_band_form()
            ssend[...] = jnp.broadcast_to(form, (8, 128))
            for k in range(1, nl):
                pltpu.make_async_remote_copy(
                    ssend, sbuf.at[l], s_sems.at[0], s_sems.at[1],
                    device_id={"lat": lax.rem(l + k, nl)}, device_id_type=MESH,
                ).start()
            sbuf[l] = ssend[...]
        acc = jnp.zeros((leg_rows, nc * two_fp), F32)
        weighted = lean and it == ITERS - 2
        sums = [jnp.zeros((rhs_ref.shape[0], 128), F32) for _ in range(10 if weighted else 4)]
        if it == 0:
            wait_bytes(leg_all.at[pl.ds(0, nl - 1)], leg_sems.at[1])
        for ch in range(lmax // chunk):
            where = pl.ds(ch * chunk, chunk)
            legs = legs_of(where)
            spread = mm(y, legs, 0, 0)
            bm = beam_ref[:, where]
            values = []
            for k in range(2):
                both = pl.ds(k * lmax + ch * chunk, chunk)
                first_lane = lane_block(k, ch * chunk)
                harm = jnp.concatenate(
                    [spread[i * two_fp + k * fp : i * two_fp + (k + 1) * fp] for i in range(nc)],
                    axis=0,
                )
                back = mm(mixt, (harm * bm).astype(BF16), 1, 0)
                if it == 0:
                    d = rhs_ref2[:, both]
                    rest = d
                else:
                    old = rhs_ref2[:, both] if it == 1 else keep[2, :, both]
                    before = rhs_ref2[:, both] if it == 1 else keep[1, :, both]
                    grown = step * old
                    put(0, sol_ref, last, both, first_lane, grown if it == 1 else keep[0, :, both] + grown)
                    rest = before - step * keep[3, :, both]
                    d = rest + ratio * old
                    put(1, res_ref, last, both, first_lane, rest)
                    put(2, dir_out, last, both, first_lane, d)
                w = prior_ref[:, where] * d + back
                put(3, w_ref, last, both, first_lane, w)
                if not (last and lean):
                    sums[0] = sums[0] + fold(d * w)
                    sums[3] = sums[3] + fold(rest * rest)
                if weighted:
                    pr, pw, pd = [prior_ref[:, where] * v for v in (rest, w, d)]
                    for i, v in enumerate(
                        (rest * pr, w * pw, d * pd, rest * pw, rest * pd, w * pd)
                    ):
                        sums[4 + i] = sums[4 + i] + fold(v)
                if not last:
                    sums[1] = sums[1] + fold(rest * w)
                    sums[2] = sums[2] + fold(w * w)
                values.append(w)
            if not last:
                acc = forward(values, where, legs, acc)
        if not last:
            tile = tile_of(acc)
            for i in range(len(sums)):
                tile = jnp.where(mark(i), total(sums[i]), tile)
            xsend[it] = tile
            share_x(it + 1)
            if lean and it == 0:
                send_full()
            if lean and it == ITERS - 2:
                place_full()

    if lean:
        wait_bytes(sbuf.at[pl.ds(0, nl - 1)], s_sems.at[1])
        form = sbuf[0]
        for i in range(1, nl):
            form = form + sbuf[i]
        step = norm / (smooth + form[0:1, 0:1])
    else:
        small_rows = lax.broadcasted_iota(jnp.int32, (8, 128), 0)
        ssend[...] = jnp.where(
            small_rows == 0, total(sums[0]), jnp.where(small_rows == 1, total(sums[3]), 0.0)
        )

        def send_s(k):
            pb, pc = peer_x(k + 1)
            pltpu.make_async_remote_copy(
                ssend, sbuf.at[me_x], s_sems.at[0], s_sems.at[1],
                device_id={"blk": pb, "comp": pc}, device_id_type=MESH,
            ).start()

        each(n_x - 1, send_s)
        sbuf[me_x] = ssend[...]
        wait_bytes(sbuf.at[pl.ds(0, n_x - 1)], s_sems.at[1])
        sums = sbuf[0]
        for i in range(1, n_x):
            sums = sums + sbuf[i]
        step = sums[1:2, 0:1] / sums[0:1, 0:1]
    step_out[...] = jnp.broadcast_to(step, (8, 128))

    wait_bytes(leg_all.at[pl.ds(0, nl - 1)], leg_sems.at[0])
    wait_bytes(gbuf.at[pl.ds(0, n_all - 1)], g_sems.at[0])
    for r in range(1, ITERS):
        wait_bytes(xbuf.at[r - 1, pl.ds(0, n_x - 1)], x_sems.at[r - 1, 0])
    if lean:
        wait_bytes(gfull.at[pl.ds(0, n_x - 1)], f_sems.at[0])
        wait_bytes(sbuf.at[pl.ds(0, nl - 1)], s_sems.at[0])
    else:
        wait_bytes(sbuf.at[pl.ds(0, n_x - 1)], s_sems.at[0])


def local(
    rhs, legendre, beam, mixing, prior, inv_noise, mask_flags, cycle_len, cycle_slot, m_values
):
    nb, nc, nl = lax.axis_size("blk"), lax.axis_size("comp"), lax.axis_size("lat")
    fl, qr, pmax = inv_noise.shape
    lmax, rb = legendre.shape[1:]
    mt = m_values.shape[0]
    comps = rhs.shape[0]
    fp = 8 * (fl // 8 + 1)
    chunk = min(512, lmax)
    lean = mt <= 8
    full = 2 * mt * mt if lean else 16
    dims = (nb, nc, nl, fl, fp, qr, rb, mt, lmax, pmax, chunk, lean)
    n_all, n_x = nb * nc * nl, nb * nc
    vm = pl.BlockSpec(memory_space=pltpu.VMEM)
    sm = pl.BlockSpec(memory_space=pltpu.SMEM)
    flat = jax.ShapeDtypeStruct((comps, 2 * lmax // 128, 128), F32)
    sol, direction, res, applied, step = pl.pallas_call(
        functools.partial(kernel, dims),
        out_shape=(flat,) * 4 + (jax.ShapeDtypeStruct((8, 128), F32),),
        in_specs=[vm] * 7 + [sm, sm, vm, sm],
        out_specs=(vm,) * 5,
        scratch_shapes=[
            pltpu.VMEM((nc * fp, lmax), F32),
            pltpu.VMEM((nc * fp, comps), F32),
            pltpu.VMEM((comps, 2 * lmax), F32),
            pltpu.VMEM((nl, rb, lmax), BF16),
            pltpu.VMEM((qr, 2, mt, pmax), F32),
            pltpu.VMEM((qr, fp, pmax), BF16),
            pltpu.VMEM((mt, 2 * mt, 128), F32),
            pltpu.VMEM((n_all, 2 * mt + rb // nl, 128), BF16),
            pltpu.VMEM((2 * mt, rb, 128), F32),
            pltpu.VMEM((rb, 2 * mt, 128), F32),
            pltpu.VMEM((full, 128), F32),
            pltpu.VMEM((n_x, full, 128), BF16),
            pltpu.VMEM((rb, full, 128), F32),
            pltpu.VMEM((full, rb, 128), F32),
            pltpu.VMEM((mt, 2 * mt + rb // nl, 128), BF16),
            pltpu.VMEM((ITERS - 1, rb, 128), F32),
            pltpu.VMEM((ITERS - 1, n_x, rb, 128), F32),
            pltpu.VMEM((8, 128), F32),
            pltpu.VMEM((n_x, 8, 128), F32),
            pltpu.VMEM((mt, rb, 128), F32),
            pltpu.VMEM((mt, rb, 128), F32),
            pltpu.VMEM((4, comps, 2 * lmax), F32),
            pltpu.SemaphoreType.DMA((2,)),
            pltpu.SemaphoreType.DMA((2,)),
            pltpu.SemaphoreType.DMA((2,)),
            pltpu.SemaphoreType.DMA((ITERS - 1, 2)),
            pltpu.SemaphoreType.DMA((2,)),
        ],
        compiler_params=pltpu.CompilerParams(collective_id=0, has_side_effects=True),
    )(
        rhs.reshape(comps, 2 * lmax // 128, 128),
        legendre[0].T,
        beam,
        mixing,
        prior,
        inv_noise,
        mask_flags.T,
        cycle_len,
        cycle_slot,
        cycle_slot[None, :],
        m_values,
    )
    step = step[0, 0]
    sol = sol + step * direction
    res = res - step * applied
    return sol.reshape(rhs.shape), res.reshape(rhs.shape)


def solution(mesh):
    in_specs = (
        P(("groups", "comp"), None, "blk", None),
        P("blk", None, "lat"),
        P(),
        P(None, "comp"),
        P("comp", None),
        P("comp", ("blk", "lat"), None),
        P("comp", ("blk", "lat")),
        P("lat"),
        P("lat"),
        P(),
    )
    out_specs = (P(("groups", "comp"), None, "blk", None), P(("groups", "comp"), None, "blk", None))
    return jax.shard_map(local, mesh=mesh, in_specs=in_specs, out_specs=out_specs, check_vma=False)
```
